128 devices in a mesh: dp: 16 (over z, x), pipe: 8 (over y, core).
Axes of the slice: x: 4, y: 4, z: 4, core: 2. Of those that a mesh axis runs over, the one named last changes fastest.
Arguments:
- tokens: bfloat16 [128, 64, 3072], P('dp'), may hold values from -40 to 40
- segments: int32 [128, 64], P('dp'), may hold values from 0 to 5, never falling along the last dimension, each value on 1 to 24 neighbouring positions
- keep_mask: int32 [128, 64], P('dp'), may hold values 0 or 1
- norm_gain: float32 [8, 3072], P('pipe'), may hold values from 0.5 to 2
- norm_bias: float32 [8, 3072], P('pipe'), may hold values from -3 to 3
- w_qkv: bfloat16 [8, 3072, 4608], P('pipe', 'dp'), may hold values from -0.109375 to 0.109375
- w_out: bfloat16 [8, 1536, 3072], P('pipe', 'dp'), may hold values from -0.15625 to 0.15625
Outputs:
- layer_outputs: bfloat16 [8, 128, 64, 3072], P('pipe', 'dp')
The draws below stay inside these ranges and needn't reach their ends.
Inputs may be any that keep to these rules, and one draw needn't show every extreme that they name: `segments`: image numbers never fall along a sequence; every image spans 1 to 24 patches and one spans exactly 24.
All inputs are finite; a program needn't handle non-finite values. No bound on the sum of `keep_mask` on one device may be relied on, other than what follows from the above.
Results may differ from the reference program's by a relative error of at most 0.013.
Values may be sent and summed in bfloat16 or wider, within the bound.
No kernel may reach another device: no remote copies, remote signals or barrier semaphores. Data moves between devices by JAX's collectives and lax.ppermute only.
A program may use at most 128 MiB of HBM per device.

```python
import math
import jax
import jax.numpy as jnp
import numpy as np
from jax import lax

D = 3072
HEADS = 24
HD = 64
GROUPS = 32
IMGS = 6
LEN = 64
INNER = 1536
SEGMOST = 24
SEQS = 128
LAYERS = 8


def draw_tokens(key, part):
    subkeys = jax.random.split(jax.random.fold_in(key, 11), 3)
    base = jnp.clip(jax.random.normal(subkeys[0], (SEQS, LEN, D), jnp.float32), -4.0, 4.0)
    row_scale = jnp.exp(jax.random.uniform(subkeys[1], (SEQS, LEN, 1), jnp.float32, math.log(0.4), math.log(4.0)))
    col_scale = jnp.exp(jax.random.uniform(subkeys[2], (1, 1, D), jnp.float32, math.log(0.5), math.log(2.0)))
    return (base * row_scale * col_scale).astype(jnp.bfloat16)


def place_ends(result, key, smallest, largest):
    shape = result.shape
    index_at = [jax.random.randint(jax.random.fold_in(key, axis), (), 0, shape[axis]) for axis in range(len(shape))]
    result = result.at[tuple(index_at)].set(smallest)
    longest = shape.index(max(shape))
    index_at[longest] = (index_at[longest] + 1) % shape[longest]
    return result.at[tuple(index_at)].set(largest)


def block_levels(key, shape, cuts, smallest, top_value):
    loudness, own = 1.0, jax.random.fold_in(key, 6)
    for axis_at, blocks in cuts:
        steps = jnp.exp(jax.random.uniform(jax.random.fold_in(own, axis_at), (blocks,), jnp.float32, smallest / len(cuts), top_value / len(cuts)))
        loudness = loudness * jnp.repeat(steps, shape[axis_at] // blocks).reshape([-1 if axis == axis_at else 1 for axis in range(len(shape))])
    return loudness


def length_profile(number_of, total, reach, skew):
    loads = [(1 << 20) // math.isqrt(standing ** skew) + 1 for standing in range(2, number_of + 1)]
    rest, given = total - reach - (number_of - 1), [1] * (number_of - 1)
    while rest > 0:
        movable = [i for i in range(number_of - 1) if given[i] < reach]
        mass, budget = sum([loads[i] for i in movable]), rest
        for i in movable:
            addition = min(reach - given[i], max(1, budget * loads[i] // mass), rest)
            given[i] = given[i] + addition
            rest = rest - addition
    return np.array([reach] + given)


def uneven_parts(rng, amount, total, bound, skew):
    if amount == 2:
        one = jax.random.randint(rng, (), max(1, total - bound), min(bound, total - 1) + 1)
        return jnp.stack([one, total - one])
    sizes = jnp.asarray(length_profile(amount, total, bound, skew), jnp.int32)
    couples = (amount - 1) // 2
    donor, taker = sizes[1:1 + 2 * couples:2], sizes[2:2 + 2 * couples:2]
    room = jnp.minimum(donor - 1, bound - taker)
    moved = jax.random.randint(jax.random.fold_in(rng, 1), (couples,), 0, 1 << 20) % (room + 1)
    sizes = sizes.at[1:1 + 2 * couples:2].set(donor - moved).at[2:2 + 2 * couples:2].set(taker + moved)
    return sizes[jax.random.permutation(jax.random.fold_in(rng, 2), amount)]


def scatter_about(own_key, dims, scale, reach, cuts=(), kind=jnp.bfloat16):
    loudness = block_levels(own_key, dims, cuts, -0.22, 0.18) if cuts else 1.0
    result = jax.random.normal(own_key, dims, jnp.float32) * scale * loudness
    return jnp.minimum(jnp.maximum(result, -reach), reach).astype(kind)


def setup_inputs(seed: int = 0) -> dict:
    arg_keys = jax.random.split(jax.random.key(seed), 8)
    return {
        "tokens": draw_tokens(jax.random.fold_in(arg_keys[7], 71), 0),
        "segments": jax.vmap(lambda own: jnp.searchsorted(jnp.cumsum(uneven_parts(own, IMGS, LEN, SEGMOST, 2)), jnp.arange(LEN), side="right"))(jax.random.split(arg_keys[1], SEQS)).reshape((SEQS, LEN)).astype(jnp.int32),
        "keep_mask": place_ends((jax.random.randint(arg_keys[2], (SEQS, LEN), 0, 8) < 7).astype(jnp.int32), jax.random.fold_in(arg_keys[2], 1), 0, 1),
        "norm_gain": jnp.clip(jnp.exp(math.log(2.0) - 1.3862944 * jax.random.uniform(arg_keys[3], (LAYERS, D), jnp.float32) ** block_levels(arg_keys[3], (LAYERS, D), ((0, 8),), -0.2, 0.2)), 0.5, 2.0),
        "norm_bias": scatter_about(arg_keys[4], (LAYERS, D), 0.5, 3.0, ((0, 8),), jnp.float32),
        "w_qkv": scatter_about(arg_keys[5], (LAYERS, D, 3 * INNER), D ** -0.5, 0.109375, ((0, 8), (1, 16))),
        "w_out": scatter_about(arg_keys[6], (LAYERS, INNER, D), INNER ** -0.5, 0.15625, ((0, 8), (1, 16))),
    }


norm_eps = 1e-05

def group_normed(stream, seg_row, keep_row, gain, bias_row):
    length = stream.shape[0]
    group_width = D // GROUPS
    values = stream.astype(jnp.float32).reshape(length, GROUPS, group_width)
    member = ((seg_row[:, None] == jnp.arange(IMGS, dtype=jnp.int32)[None, :]) & (keep_row[:, None] > 0)).astype(jnp.float32)
    counted = jnp.maximum(lax.optimization_barrier(jnp.sum(member, axis=0)) * group_width, 1.0)
    img_sum = jnp.dot(member.T, lax.optimization_barrier(jnp.sum(values, axis=2)), precision=lax.Precision.HIGHEST)
    img_mean = img_sum / counted[:, None]
    tok_mean = jnp.dot(member, img_mean, precision=lax.Precision.HIGHEST)
    centred = values - tok_mean[:, :, None]
    img_var = jnp.dot(member.T, lax.optimization_barrier(jnp.sum(centred * centred, axis=2)), precision=lax.Precision.HIGHEST) / counted[:, None]
    tok_var = jnp.dot(member, img_var, precision=lax.Precision.HIGHEST)
    normed = (centred * lax.rsqrt(tok_var + norm_eps)[:, :, None]).reshape(length, D)
    normed = (normed * gain[None, :] + bias_row[None, :]) * keep_row[:, None].astype(jnp.float32)
    return normed.astype(jnp.bfloat16)

def one_layer(stream, seg_row, keep_row, gain, bias_row, qkv_weight, out_weight):
    length = stream.shape[0]
    normed = group_normed(stream, seg_row, keep_row, gain, bias_row)
    projected = jnp.dot(normed, qkv_weight, preferred_element_type=jnp.float32)
    query_rows = projected[:, :INNER].reshape(length, HEADS, HD)
    key_rows = projected[:, INNER:2 * INNER].reshape(length, HEADS, HD)
    value_rows = projected[:, 2 * INNER:].reshape(length, HEADS, HD).astype(jnp.bfloat16)
    query_rows = (query_rows * lax.rsqrt(lax.optimization_barrier(jnp.mean(query_rows * query_rows, axis=2, keepdims=True)) + 1e-06)).astype(jnp.bfloat16)
    key_rows = (key_rows * lax.rsqrt(lax.optimization_barrier(jnp.mean(key_rows * key_rows, axis=2, keepdims=True)) + 1e-06)).astype(jnp.bfloat16)
    scores = jnp.einsum('qhd,khd->hqk', query_rows.astype(jnp.float32), key_rows.astype(jnp.float32)) / math.sqrt(HD)
    keep_float = keep_row.astype(jnp.float32)
    allowed = (seg_row[:, None] == seg_row[None, :]).astype(jnp.float32) * keep_float[:, None] * keep_float[None, :]
    expo = jnp.exp(scores) * allowed[None, :, :]
    denominator = lax.optimization_barrier(jnp.sum(expo, axis=2)) + (1.0 - keep_float)[None, :]
    probs = (expo / denominator[:, :, None]).astype(jnp.bfloat16)
    attended = jnp.einsum('hqk,khd->qhd', probs.astype(jnp.float32), value_rows.astype(jnp.float32))
    attended = attended.reshape(length, INNER).astype(jnp.bfloat16)
    branch = jnp.dot(attended, out_weight, preferred_element_type=jnp.float32)
    return (stream.astype(jnp.float32) + branch).astype(jnp.bfloat16)

def reference(tokens, segments, keep_mask, norm_gain, norm_bias, w_qkv, w_out):
    stream = tokens
    saved = []
    for layer_no in range(LAYERS):

        def apply_one(stream_row, seg_row, keep_row):
            return one_layer(stream_row, seg_row, keep_row, norm_gain[layer_no], norm_bias[layer_no], w_qkv[layer_no], w_out[layer_no])
        stream = lax.map(lambda packed: apply_one(packed[0], packed[1], packed[2]), (stream, segments, keep_mask))
        saved.append(stream)
    return jnp.stack(saved)
```

```python
import math

import jax
import jax.numpy as jnp
from jax import lax
from jax.experimental import pallas as pl
from jax.experimental.pallas import tpu as pltpu
from jax.sharding import PartitionSpec as P

D = 3072
HEADS = 24
HD = 64
GROUPS = 32
IMGS = 6
INNER = 1536
WIDTH = D // GROUPS
LEN = 64
PER = 2
ROWS = PER * LEN
BLOCK = 256
BF = jnp.bfloat16
F32 = jnp.float32

norm_eps = 1e-05


def parts(value, count):
    found = []
    for at in range(count):
        piece = value.astype(BF)
        found.append(piece)
        if at + 1 < count:
            value = value - piece.astype(F32)
    return found


def dot(a, b):
    return jnp.dot(a, b, preferred_element_type=F32)


def dot_nt(a, b):
    return lax.dot_general(a, b, (((1,), (1,)), ((), ())), preferred_element_type=F32)


def group_normed(x, code_c, code_r, gain, bias):
    slots = PER * 8
    slot = lax.broadcasted_iota(jnp.int32, (ROWS, slots), 1)
    row = lax.broadcasted_iota(jnp.int32, (ROWS, slots), 0)
    member = ((code_c == slot % 8) & (row // LEN == slot // 8)).astype(F32)
    member_t = jnp.concatenate(
        [
            jnp.concatenate(
                [
                    (code_r[at] == lax.broadcasted_iota(jnp.int32, (8, LEN), 0)).astype(BF)
                    if at == seq
                    else jnp.zeros((8, LEN), BF)
                    for at in range(PER)
                ],
                axis=1,
            )
            for seq in range(PER)
        ],
        axis=0,
    )
    ch = lax.broadcasted_iota(jnp.int32, (D, GROUPS), 0)
    low = lax.broadcasted_iota(jnp.int32, (D, GROUPS), 1) * WIDTH
    to_group = ((ch >= low) & (ch < low + WIDTH)).astype(BF)
    ch = lax.broadcasted_iota(jnp.int32, (GROUPS * 3, D), 1)
    low = lax.broadcasted_iota(jnp.int32, (GROUPS * 3, D), 0) % GROUPS * WIDTH
    to_channel = ((ch >= low) & (ch < low + WIDTH)).astype(BF)
    counted = jnp.maximum(jnp.sum(member_t.astype(F32), axis=1, keepdims=True) * WIDTH, 1.0)
    member3 = jnp.concatenate([member] * 3, axis=1).astype(BF)

    def group_mean(per_image):
        sums = dot(jnp.concatenate(parts(per_image, 3), axis=0), to_group)
        return (sums[:slots] + sums[slots : 2 * slots] + sums[2 * slots :]) / counted

    def of_tokens(per_image):
        return dot(member3, jnp.concatenate(parts(per_image, 3), axis=0))

    def of_channels(per_group):
        return dot(jnp.concatenate(parts(per_group, 3), axis=1), to_channel)

    mean = group_mean(dot(member_t, x))
    centred = x.astype(F32) - of_channels(of_tokens(mean))
    square = parts(centred * centred, 2)
    var = group_mean(dot(member_t, square[0]) + dot(member_t, square[1]))
    inverse = lax.rsqrt(of_tokens(var) + norm_eps)
    kept = (code_c >= 0).astype(F32)
    return ((centred * of_channels(inverse) * gain + bias) * kept).astype(BF)


def tick_kernel(
    now_ref, at_ref, incoming_ref, tokens_ref, code_c_ref, code_r_ref, gain_ref, bias_ref, w_ref, saved_in_ref,
    out_ref, saved_ref, x_ref, normed_ref, attended_ref, y_ref, held_ref, sem, w_sem, out_sem,
):
    del saved_in_ref
    mine = now_ref[0] - at_ref[0]
    micros = tokens_ref.shape[0]
    micro = jnp.clip(mine, 0, micros - 1)

    def load(j):
        cols = pl.ds(j % 6 * BLOCK, BLOCK)
        rows = pl.ds(0, 576) if j < 6 else pl.ds(576, 192)
        return pltpu.make_async_copy(w_ref.at[:, rows, cols], held_ref.at[:, rows, cols], w_sem.at[j])

    def wq(part, j):
        return held_ref[:, part * 192 : (part + 1) * 192, j * BLOCK : (j + 1) * BLOCK].reshape(D, BLOCK)

    def wo(c):
        top = 576 + 96 * (c // 6)
        return held_ref[:, top : top + 96, c % 6 * BLOCK : (c % 6 + 1) * BLOCK].reshape(INNER, BLOCK)

    @pl.when((mine >= 0) & (mine < micros))
    def _():
        @pl.when(at_ref[0] == 0)
        def _():
            pltpu.make_async_copy(tokens_ref.at[micro], x_ref, sem.at[0]).start()

        @pl.when(at_ref[0] != 0)
        def _():
            pltpu.make_async_copy(incoming_ref, x_ref, sem.at[0]).start()

        for j in range(12):
            load(j).start()
        pltpu.make_async_copy(incoming_ref, x_ref, sem.at[0]).wait()
        code_c = code_c_ref[micro]
        code_r = [code_r_ref[micro, at : at + 1, :] for at in range(PER)]
        normed_ref[...] = group_normed(x_ref[...], code_c, code_r, gain_ref[...], bias_ref[...])
        head_r = lax.broadcasted_iota(jnp.int32, (BLOCK, BLOCK), 0) // HD
        head_c = lax.broadcasted_iota(jnp.int32, (BLOCK, BLOCK), 1) // HD
        same = head_r == head_c
        one = same.astype(BF)
        same2 = jnp.concatenate([one, one], axis=0)
        zero = jnp.zeros((BLOCK, BLOCK), BF)
        allowed = []
        for seq in range(PER):
            own = code_c[seq * LEN : (seq + 1) * LEN]
            tile = ((own == code_r[seq]) & (own >= 0)).astype(F32)
            allowed.append(jnp.concatenate([tile] * 4, axis=1))
        dropped = (code_c < 0).astype(F32)

        def head_normed(rows):
            square = dot(jnp.concatenate(parts(rows * rows, 2), axis=1), same2) * (1.0 / HD)
            return (rows * lax.rsqrt(square + 1e-06)).astype(BF)

        normed = normed_ref[...]
        for j in range(6):
            load(j).wait()
            query = head_normed(dot(normed, wq(0, j)))
            key = head_normed(dot(normed, wq(1, j)))
            value = dot(normed, wq(2, j)).astype(BF)
            for seq in range(PER):
                rows = slice(seq * LEN, (seq + 1) * LEN)
                key_bd = jnp.where(same, jnp.concatenate([key[rows]] * 4, axis=0), zero)
                value_bd = jnp.where(same, jnp.concatenate([value[rows]] * 4, axis=0), zero)
                scores = dot_nt(query[rows], key_bd) * (1.0 / math.sqrt(HD))
                expo = jnp.exp(scores) * allowed[seq]
                total = dot(jnp.concatenate(parts(expo, 2), axis=1), same2) + dropped[rows]
                probs = (expo / total).astype(BF)
                attended_ref[rows, j * BLOCK : (j + 1) * BLOCK] = dot(probs, value_bd).astype(BF)
        attended = attended_ref[...]
        for j in range(6):
            load(6 + j).wait()
            for c in (j, j + 6):
                cols = slice(c * BLOCK, (c + 1) * BLOCK)
                y_ref[:, cols] = (x_ref[:, cols].astype(F32) + dot(attended, wo(c))).astype(BF)
        copies = [
            pltpu.make_async_copy(y_ref, out_ref, out_sem.at[0]),
            pltpu.make_async_copy(y_ref, saved_ref.at[micro], out_sem.at[1]),
        ]
        for copy in copies:
            copy.start()
        for copy in copies:
            copy.wait()


def tick(now, at, incoming, tokens, code_c, code_r, gain, bias, weights, saved):
    whole = pl.BlockSpec(memory_space=pltpu.VMEM)
    anywhere = pl.BlockSpec(memory_space=pl.ANY)
    scalar = pl.BlockSpec(memory_space=pltpu.SMEM)
    return pl.pallas_call(
        tick_kernel,
        out_shape=(jax.ShapeDtypeStruct((ROWS, D), BF), jax.ShapeDtypeStruct(saved.shape, BF)),
        in_specs=[scalar, scalar, anywhere, anywhere, whole, whole, whole, whole, anywhere, anywhere],
        out_specs=(anywhere, anywhere),
        scratch_shapes=[
            pltpu.VMEM((ROWS, D), BF),
            pltpu.VMEM((ROWS, D), BF),
            pltpu.VMEM((ROWS, INNER), BF),
            pltpu.VMEM((ROWS, D), BF),
            pltpu.VMEM(weights.shape, BF),
            pltpu.SemaphoreType.DMA((1,)),
            pltpu.SemaphoreType.DMA((12,)),
            pltpu.SemaphoreType.DMA((2,)),
        ],
        input_output_aliases={9: 1},
        compiler_params=pltpu.CompilerParams(vmem_limit_bytes=58 << 20),
    )(now, at, incoming, tokens, code_c, code_r, gain, bias, weights, saved)


def local(tokens, segments, keep_mask, norm_gain, norm_bias, w_qkv, w_out):
    section = lax.axis_index("pipe")
    sections = lax.axis_size("pipe")
    micro = tokens.shape[0] // PER
    qkv, out = w_qkv[0], w_out[0]
    packed = jnp.concatenate(
        [qkv[:, i * INNER : (i + 1) * INNER] for i in range(3)] + [out[:, i * INNER : (i + 1) * INNER] for i in range(2)],
        axis=0,
    )
    weights = lax.all_gather(packed, "dp", axis=0)
    code = jnp.where(keep_mask > 0, segments, -1)
    code_c = code.reshape(micro, ROWS, 1)
    code_r = code.reshape(micro, PER, LEN)
    shaped = tokens.reshape(micro, ROWS, D)
    saved = jnp.zeros(shaped.shape, BF)
    incoming = jnp.zeros((ROWS, D), BF)
    steps = [(i, i + 1) for i in range(sections - 1)]
    at = section.reshape(1)

    def body(now, carried):
        incoming, saved = carried
        result, saved = tick(now.reshape(1), at, incoming, shaped, code_c, code_r, norm_gain, norm_bias, weights, saved)
        return lax.ppermute(result, "pipe", steps), saved

    _, saved = lax.fori_loop(0, micro + sections - 1, body, (incoming, saved))
    return saved.reshape((1,) + tokens.shape)


def solution(mesh):
    placed = (
        P("dp", None, None),
        P("dp", None),
        P("dp", None),
        P("pipe", None),
        P("pipe", None),
        P("pipe", "dp", None),
        P("pipe", "dp", None),
    )
    return jax.shard_map(
        local, mesh=mesh, in_specs=placed, out_specs=P("pipe", "dp", None, None), check_vma=False
    )
```

```python
import functools
import math

import jax
import jax.numpy as jnp
from jax import lax
from jax.experimental import pallas as pl
from jax.experimental.pallas import tpu as pltpu
from jax.sharding import PartitionSpec as P

D = 3072
HEADS = 24
HD = 64
GROUPS = 32
IMGS = 6
INNER = 1536
WIDTH = D // GROUPS
LEN = 64
PER = 2
ROWS = PER * LEN
BLOCK = 256
BF = jnp.bfloat16
F32 = jnp.float32

norm_eps = 1e-05


def parts(value, count):
    found = []
    for at in range(count):
        piece = value.astype(BF)
        found.append(piece)
        if at + 1 < count:
            value = value - piece.astype(F32)
    return found


def dot(a, b):
    return jnp.dot(a, b, preferred_element_type=F32)


def dot_nt(a, b):
    return lax.dot_general(a, b, (((1,), (1,)), ((), ())), preferred_element_type=F32)


def group_normed(x, code_c, code_r, gain, bias, to_channel):
    kept = code_c >= 0
    together = ((code_c == code_r) & kept).astype(BF)
    counted = jnp.maximum(jnp.sum(together.astype(F32), axis=1, keepdims=True) * WIDTH, 1.0)

    def image_mean(rows):
        sums = dot_nt(rows, to_channel[:GROUPS])
        sums = dot(together, jnp.concatenate(parts(sums, 3), axis=1))
        return (sums[:, :GROUPS] + sums[:, GROUPS : 2 * GROUPS] + sums[:, 2 * GROUPS :]) / counted

    def of_channels(per_group):
        return dot(jnp.concatenate(parts(per_group, 3), axis=1), to_channel)

    centred = x.astype(F32) - of_channels(image_mean(x))
    inverse = lax.rsqrt(image_mean((centred * centred).astype(BF)) + norm_eps)
    return ((centred * of_channels(inverse) * gain + bias) * kept.astype(F32)).astype(BF)


def tick_kernel(now, at_ref, incoming_ref, tokens_ref, code_c_ref, code_r_ref, gain_ref, bias_ref, groups_ref, w_ref, *rest):
    out_ref, saved_ref, x_ref, normed_ref, attended_ref, sem, out_sem = rest[-7:]
    mine = now - at_ref[0]
    micros = tokens_ref.shape[0]
    micro = jnp.clip(mine, 0, micros - 1)

    def wq(part, j):
        return w_ref[:, part * 192 : (part + 1) * 192, j * BLOCK : (j + 1) * BLOCK].reshape(D, BLOCK)

    def wo(c):
        top = 576 + 96 * (c // 6)
        return w_ref[:, top : top + 96, c % 6 * BLOCK : (c % 6 + 1) * BLOCK].reshape(INNER, BLOCK)

    def save(c):
        cols = pl.ds(c * BLOCK, BLOCK)
        return pltpu.make_async_copy(out_ref.at[:, cols], saved_ref.at[micro, :, cols], out_sem.at[c])

    @pl.when((mine >= 0) & (mine < micros))
    def _():
        @pl.when(at_ref[0] == 0)
        def _():
            copy = pltpu.make_async_copy(tokens_ref.at[micro], x_ref, sem.at[0])
            copy.start()
            copy.wait()

        @pl.when(at_ref[0] != 0)
        def _():
            x_ref[...] = incoming_ref[...]

        code_c = code_c_ref[micro]
        code_r = code_r_ref[micro]
        normed_ref[...] = group_normed(x_ref[...], code_c, code_r, gain_ref[...], bias_ref[...], groups_ref[...])
        head_r = lax.broadcasted_iota(jnp.int32, (BLOCK, BLOCK), 0) // HD
        head_c = lax.broadcasted_iota(jnp.int32, (BLOCK, BLOCK), 1) // HD
        same = head_r == head_c
        one = same.astype(BF)
        zero = jnp.zeros((BLOCK, BLOCK), BF)
        allowed = []
        for seq in range(PER):
            own = code_c[seq * LEN : (seq + 1) * LEN]
            tile = ((own == code_r[:, seq * LEN : (seq + 1) * LEN]) & (own >= 0)).astype(F32)
            allowed.append(jnp.concatenate([tile] * 4, axis=1))
        dropped = (code_c < 0).astype(F32)
        normed = normed_ref[...]
        def project(j):
            return dot(normed, wq(0, j)), dot(normed, wq(1, j)), dot(normed, wq(2, j))

        def attend(j, query, key, value):
            pair = jnp.concatenate([query, key], axis=0)
            square = dot((pair * pair).astype(BF), one) * (1.0 / HD)
            pair = pair * lax.rsqrt(square + 1e-06)
            query = (pair[:ROWS] * (1.0 / math.sqrt(HD))).astype(BF)
            key = pair[ROWS:].astype(BF)
            value = value.astype(BF)
            for seq in range(PER):
                rows = slice(seq * LEN, (seq + 1) * LEN)
                key_bd = jnp.where(same, jnp.concatenate([key[rows]] * 4, axis=0), zero)
                value_bd = jnp.where(same, jnp.concatenate([value[rows]] * 4, axis=0), zero)
                expo = (jnp.exp(dot_nt(query[rows], key_bd)) * allowed[seq]).astype(BF)
                both = dot(expo, jnp.concatenate([value_bd, one], axis=1))
                found = both[:, :BLOCK] / (both[:, BLOCK:] + dropped[rows])
                attended_ref[rows, j * BLOCK : (j + 1) * BLOCK] = found.astype(BF)

        ready = project(0)
        for j in range(6):
            following = project(j + 1) if j < 5 else None
            attend(j, *ready)
            ready = following
        attended = attended_ref[...]
        for j in range(6):
            for c in (j, j + 6):
                cols = slice(c * BLOCK, (c + 1) * BLOCK)
                out_ref[:, cols] = (x_ref[:, cols].astype(F32) + dot(attended, wo(c))).astype(BF)
                save(c).start()
        for c in range(12):
            save(c).wait()


def tick(now, at, incoming, tokens, code_c, code_r, gain, bias, groups, weights, saved):
    whole = pl.BlockSpec(memory_space=pltpu.VMEM)
    anywhere = pl.BlockSpec(memory_space=pl.ANY)
    scalar = pl.BlockSpec(memory_space=pltpu.SMEM)
    return pl.pallas_call(
        functools.partial(tick_kernel, now),
        out_shape=(jax.ShapeDtypeStruct((ROWS, D), BF), jax.ShapeDtypeStruct(tokens.shape, BF)),
        in_specs=[scalar, whole, anywhere, whole, whole, whole, whole, whole, whole] + [anywhere] * len(saved),
        out_specs=(whole, anywhere),
        scratch_shapes=[
            pltpu.VMEM((ROWS, D), BF),
            pltpu.VMEM((ROWS, D), BF),
            pltpu.VMEM((ROWS, INNER), BF),
            pltpu.SemaphoreType.DMA((1,)),
            pltpu.SemaphoreType.DMA((12,)),
        ],
        input_output_aliases={9: 1} if saved else {},
        compiler_params=pltpu.CompilerParams(vmem_limit_bytes=18 << 20),
    )(at, incoming, tokens, code_c, code_r, gain, bias, groups, weights, *saved)


def local(tokens, segments, keep_mask, norm_gain, norm_bias, w_qkv, w_out):
    section = lax.axis_index("pipe")
    sections = lax.axis_size("pipe")
    micro = tokens.shape[0] // PER
    qkv, out = w_qkv[0], w_out[0]
    packed = jnp.concatenate(
        [qkv[:, i * INNER : (i + 1) * INNER] for i in range(3)] + [out[:, i * INNER : (i + 1) * INNER] for i in range(2)],
        axis=0,
    )
    weights = lax.all_gather(packed, "dp", axis=0)
    place = lax.broadcasted_iota(jnp.int32, segments.shape, 0) % PER * IMGS
    code = jnp.where(keep_mask > 0, segments + place, -1)
    code_c = code.reshape(micro, ROWS, 1)
    code_r = code.reshape(micro, 1, ROWS)
    owner = lax.broadcasted_iota(jnp.int32, (GROUPS * 3, D), 0) % GROUPS
    groups = (lax.broadcasted_iota(jnp.int32, (GROUPS * 3, D), 1) // WIDTH == owner).astype(BF)
    shaped = tokens.reshape(micro, ROWS, D)
    saved = []
    incoming = shaped[0]
    steps = [(i, i + 1) for i in range(sections - 1)]
    at = section.reshape(1)

    weights = pltpu.with_memory_space_constraint(weights, pltpu.VMEM)
    for now in range(micro + sections - 1):
        result, *saved = tick(now, at, incoming, shaped, code_c, code_r, norm_gain, norm_bias, groups, weights, saved)
        if now < micro + sections - 2:
            result = pltpu.with_memory_space_constraint(result, pltpu.VMEM)
            incoming = pltpu.with_memory_space_constraint(lax.ppermute(result, "pipe", steps), pltpu.VMEM)
    return saved[0].reshape((1,) + tokens.shape)


def solution(mesh):
    placed = (
        P("dp", None, None),
        P("dp", None),
        P("dp", None),
        P("pipe", None),
        P("pipe", None),
        P("pipe", "dp", None),
        P("pipe", "dp", None),
    )
    return jax.shard_map(
        local, mesh=mesh, in_specs=placed, out_specs=P("pipe", "dp", None, None), check_vma=False
    )
```

```python
import functools
import math

import jax
import jax.numpy as jnp
from jax import lax
from jax.experimental import pallas as pl
from jax.experimental.pallas import tpu as pltpu
from jax.sharding import PartitionSpec as P

D = 3072
HEADS = 24
HD = 64
GROUPS = 32
IMGS = 6
INNER = 1536
WIDTH = D // GROUPS
LEN = 64
PER = 2
ROWS = PER * LEN
BLOCK = 256
BF = jnp.bfloat16
F32 = jnp.float32

norm_eps = 1e-05


def parts(value, count):
    found = []
    for at in range(count):
        piece = value.astype(BF)
        found.append(piece)
        if at + 1 < count:
            value = value - piece.astype(F32)
    return found


def dot(a, b):
    return jnp.dot(a, b, preferred_element_type=F32)


def dot_nt(a, b):
    return lax.dot_general(a, b, (((1,), (1,)), ((), ())), preferred_element_type=F32)


def group_normed(x, code_c, code_r, gain, bias, to_channel):
    kept = code_c >= 0
    together = ((code_c == code_r) & kept).astype(BF)
    counted = jnp.maximum(jnp.sum(together.astype(F32), axis=1, keepdims=True) * WIDTH, 1.0)

    def image_mean(rows):
        sums = dot_nt(rows, to_channel[:GROUPS])
        sums = dot(together, jnp.concatenate(parts(sums, 3), axis=1))
        return (sums[:, :GROUPS] + sums[:, GROUPS : 2 * GROUPS] + sums[:, 2 * GROUPS :]) / counted

    def of_channels(per_group):
        return dot(jnp.concatenate(parts(per_group, 3), axis=1), to_channel)

    centred = x.astype(F32) - of_channels(image_mean(x))
    inverse = lax.rsqrt(image_mean((centred * centred).astype(BF)) + norm_eps)
    return ((centred * of_channels(inverse) * gain + bias) * kept.astype(F32)).astype(BF)


def tick_kernel(now, at_ref, incoming_ref, tokens_ref, code_c_ref, code_r_ref, gain_ref, bias_ref, groups_ref, w_ref, *rest):
    out_ref, saved_ref, x_ref, normed_ref, attended_ref, sem, out_sem = rest[-7:]
    mine = now - at_ref[0]
    micros = tokens_ref.shape[0]
    micro = jnp.clip(mine, 0, micros - 1)

    def wq(part, j):
        return w_ref[:, part * 192 : (part + 1) * 192, j * BLOCK : (j + 1) * BLOCK].reshape(D, BLOCK)

    def wo(c):
        top = 576 + 96 * (c // 6)
        return w_ref[:, top : top + 96, c % 6 * BLOCK : (c % 6 + 1) * BLOCK].reshape(INNER, BLOCK)

    def save(c):
        cols = pl.ds(c * BLOCK, BLOCK)
        return pltpu.make_async_copy(out_ref.at[:, cols], saved_ref.at[micro, :, cols], out_sem.at[c])

    @pl.when((mine >= 0) & (mine < micros))
    def _():
        @pl.when(at_ref[0] == 0)
        def _():
            copy = pltpu.make_async_copy(tokens_ref.at[micro], x_ref, sem.at[0])
            copy.start()
            copy.wait()

        @pl.when(at_ref[0] != 0)
        def _():
            x_ref[...] = incoming_ref[...]

        code_c = code_c_ref[micro]
        code_r = code_r_ref[micro]
        normed_ref[...] = group_normed(x_ref[...], code_c, code_r, gain_ref[...], bias_ref[...], groups_ref[...])
        head_r = lax.broadcasted_iota(jnp.int32, (BLOCK, BLOCK), 0) // HD
        head_c = lax.broadcasted_iota(jnp.int32, (BLOCK, BLOCK), 1) // HD
        same = head_r == head_c
        one = same.astype(BF)
        zero = jnp.zeros((BLOCK, BLOCK), BF)
        allowed = []
        for seq in range(PER):
            own = code_c[seq * LEN : (seq + 1) * LEN]
            tile = ((own == code_r[:, seq * LEN : (seq + 1) * LEN]) & (own >= 0)).astype(F32)
            allowed.append(jnp.concatenate([tile] * 4, axis=1))
        dropped = (code_c < 0).astype(F32)
        normed = normed_ref[...]
        def project(j):
            return dot(normed, wq(0, j)), dot(normed, wq(1, j)), dot(normed, wq(2, j))

        def attend(j, query, key, value):
            pair = jnp.concatenate([query, key], axis=0)
            square = dot((pair * pair).astype(BF), one) * (1.0 / HD)
            pair = pair * lax.rsqrt(square + 1e-06)
            query = (pair[:ROWS] * (1.0 / math.sqrt(HD))).astype(BF)
            key = pair[ROWS:].astype(BF)
            value = value.astype(BF)
            for seq in range(PER):
                rows = slice(seq * LEN, (seq + 1) * LEN)
                key_bd = jnp.where(same, jnp.concatenate([key[rows]] * 4, axis=0), zero)
                value_bd = jnp.where(same, jnp.concatenate([value[rows]] * 4, axis=0), zero)
                expo = (jnp.exp(dot_nt(query[rows], key_bd)) * allowed[seq]).astype(BF)
                both = dot(expo, jnp.concatenate([value_bd, one], axis=1))
                found = both[:, :BLOCK] / (both[:, BLOCK:] + dropped[rows])
                attended_ref[rows, j * BLOCK : (j + 1) * BLOCK] = found.astype(BF)

        ready = project(0)
        for j in range(6):
            following = project(j + 1) if j < 5 else None
            attend(j, *ready)
            ready = following
        attended = attended_ref[...]
        for j in range(6):
            for c in (j, j + 6):
                cols = slice(c * BLOCK, (c + 1) * BLOCK)
                out_ref[:, cols] = (x_ref[:, cols].astype(F32) + dot(attended, wo(c))).astype(BF)
                save(c).start()
        for c in range(12):
            save(c).wait()


def tick(now, at, incoming, tokens, code_c, code_r, gain, bias, groups, weights, saved):
    whole = pl.BlockSpec(memory_space=pltpu.VMEM)
    anywhere = pl.BlockSpec(memory_space=pl.ANY)
    scalar = pl.BlockSpec(memory_space=pltpu.SMEM)
    return pl.pallas_call(
        functools.partial(tick_kernel, now),
        out_shape=(pltpu.VMEM((ROWS, D), BF), jax.ShapeDtypeStruct(tokens.shape, BF)),
        in_specs=[scalar, whole, anywhere, whole, whole, whole, whole, whole, whole] + [anywhere] * len(saved),
        out_specs=(whole, anywhere),
        scratch_shapes=[
            pltpu.VMEM((ROWS, D), BF),
            pltpu.VMEM((ROWS, D), BF),
            pltpu.VMEM((ROWS, INNER), BF),
            pltpu.SemaphoreType.DMA((1,)),
            pltpu.SemaphoreType.DMA((12,)),
        ],
        input_output_aliases={9: 1} if saved else {},
        compiler_params=pltpu.CompilerParams(vmem_limit_bytes=18 << 20),
    )(at, incoming, tokens, code_c, code_r, gain, bias, groups, weights, *saved)


SIDE = 4


def moved(value, dz, dx):
    steps = [
        (z * SIDE + x, (z + dz) % SIDE * SIDE + (x + dx) % SIDE) for z in range(SIDE) for x in range(SIDE)
    ]
    return lax.ppermute(value, "dp", steps)


def ring(own, dz, dx):
    half = own.shape[0] // 2
    before = moved(own, dz, dx)
    after = moved(own, -dz, -dx)
    return [own, before, after, moved(before[:half], dz, dx), moved(after[half:], -dz, -dx)]


def load_kernel(at_ref, *refs):
    pieces, out_ref, sem = refs[:10], refs[10], refs[11]
    rows = out_ref.shape[1] // 2
    place = (at_ref[0] // SIDE, at_ref[0] % SIDE)
    copies = []
    for color in range(2):
        for far, far_step in enumerate((0, SIDE - 1, 1, 2)):
            for near, near_step in enumerate((0, SIDE - 1, 1, 2)):
                if far < 3:
                    source = pieces[5 * color + far].at[pl.ds(near * rows, rows)]
                else:
                    source = pieces[5 * color + 3 + near // 2].at[pl.ds(near % 2 * rows, rows)]
                z = place[0] + (far_step if color == 0 else near_step)
                x = place[1] + (near_step if color == 0 else far_step)
                target = out_ref.at[z % SIDE * SIDE + x % SIDE, pl.ds(color * rows, rows)]
                copies.append(pltpu.make_async_copy(source, target, sem.at[len(copies)]))
    for copy in copies:
        copy.start()
    for copy in copies:
        copy.wait()


def gathered(packed):
    rows = packed.shape[0] // 2
    first = [ring(packed[:rows], 0, 1), ring(packed[rows:], 1, 0)]
    second = [ring(jnp.concatenate(first[0]), 1, 0), ring(jnp.concatenate(first[1]), 0, 1)]
    weights = pl.pallas_call(
        load_kernel,
        out_shape=pltpu.VMEM((SIDE * SIDE, *packed.shape), BF),
        in_specs=[pl.BlockSpec(memory_space=pltpu.SMEM)] + [pl.BlockSpec(memory_space=pl.ANY)] * 10,
        out_specs=pl.BlockSpec(memory_space=pltpu.VMEM),
        scratch_shapes=[pltpu.SemaphoreType.DMA((32,))],
        compiler_params=pltpu.CompilerParams(vmem_limit_bytes=18 << 20),
    )(lax.axis_index("dp").reshape(1), *second[0], *second[1])
    return pltpu.with_memory_space_constraint(weights, pltpu.VMEM)


def local(tokens, segments, keep_mask, norm_gain, norm_bias, w_qkv, w_out):
    section = lax.axis_index("pipe")
    sections = lax.axis_size("pipe")
    micro = tokens.shape[0] // PER
    qkv, out = w_qkv[0], w_out[0]
    packed = jnp.concatenate(
        [qkv[:, i * INNER : (i + 1) * INNER] for i in range(3)] + [out[:, i * INNER : (i + 1) * INNER] for i in range(2)],
        axis=0,
    )
    weights = gathered(packed)
    place = lax.broadcasted_iota(jnp.int32, segments.shape, 0) % PER * IMGS
    code = jnp.where(keep_mask > 0, segments + place, -1)
    code_c = code.reshape(micro, ROWS, 1)
    code_r = code.reshape(micro, 1, ROWS)
    owner = lax.broadcasted_iota(jnp.int32, (GROUPS * 3, D), 0) % GROUPS
    groups = (lax.broadcasted_iota(jnp.int32, (GROUPS * 3, D), 1) // WIDTH == owner).astype(BF)
    shaped = tokens.reshape(micro, ROWS, D)
    saved = []
    incoming = shaped[0]
    steps = [(i, i + 1) for i in range(sections - 1)]
    at = section.reshape(1)
    fixed = [
        pltpu.with_memory_space_constraint(part, pltpu.VMEM) for part in (code_c, code_r, norm_gain, norm_bias, groups)
    ]

    for now in range(micro + sections - 1):
        result, *saved = tick(now, at, incoming, shaped, *fixed, weights, saved)
        if now < micro + sections - 2:
            incoming = pltpu.with_memory_space_constraint(lax.ppermute(result, "pipe", steps), pltpu.VMEM)
    return saved[0].reshape((1,) + tokens.shape)


def solution(mesh):
    placed = (
        P("dp", None, None),
        P("dp", None),
        P("dp", None),
        P("pipe", None),
        P("pipe", None),
        P("pipe", "dp", None),
        P("pipe", "dp", None),
    )
    return jax.shard_map(
        local, mesh=mesh, in_specs=placed, out_specs=P("pipe", "dp", None, None), check_vma=False
    )
```

```python
import functools
import math

import jax
import jax.numpy as jnp
from jax import lax
from jax.experimental import pallas as pl
from jax.experimental.pallas import tpu as pltpu
from jax.sharding import PartitionSpec as P

D = 3072
HEADS = 24
HD = 64
GROUPS = 32
IMGS = 6
INNER = 1536
WIDTH = D // GROUPS
LEN = 64
PER = 2
ROWS = PER * LEN
BLOCK = 256
BF = jnp.bfloat16
F32 = jnp.float32

norm_eps = 1e-05


def parts(value, count):
    found = []
    for at in range(count):
        piece = value.astype(BF)
        found.append(piece)
        if at + 1 < count:
            value = value - piece.astype(F32)
    return found


def dot(a, b):
    return jnp.dot(a, b, preferred_element_type=F32)


def dot_nt(a, b):
    return lax.dot_general(a, b, (((1,), (1,)), ((), ())), preferred_element_type=F32)


def group_normed(x, code_c, code_r, gain, bias, to_channel):
    kept = code_c >= 0
    together = ((code_c == code_r) & kept).astype(BF)
    counted = jnp.maximum(jnp.sum(together.astype(F32), axis=1, keepdims=True) * WIDTH, 1.0)

    def image_mean(rows):
        sums = dot_nt(rows, to_channel[:GROUPS])
        sums = dot(together, jnp.concatenate(parts(sums, 3), axis=1))
        return (sums[:, :GROUPS] + sums[:, GROUPS : 2 * GROUPS] + sums[:, 2 * GROUPS :]) / counted

    def of_channels(per_group):
        return dot(jnp.concatenate(parts(per_group, 3), axis=1), to_channel)

    centred = x.astype(F32) - of_channels(image_mean(x))
    inverse = lax.rsqrt(image_mean((centred * centred).astype(BF)) + norm_eps)
    return ((centred * of_channels(inverse) * gain + bias) * kept.astype(F32)).astype(BF)


def tick_kernel(now, at_ref, incoming_ref, tokens_ref, code_c_ref, code_r_ref, gain_ref, bias_ref, groups_ref, w_ref, *rest):
    out_ref, saved_ref, x_ref, normed_ref, attended_ref, sem, out_sem = rest[-7:]
    mine = now - at_ref[0]
    micros = tokens_ref.shape[0]
    micro = jnp.clip(mine, 0, micros - 1)

    def wq(part, j):
        return w_ref[:, part * 192 : (part + 1) * 192, j * BLOCK : (j + 1) * BLOCK].reshape(D, BLOCK)

    def wo(c):
        top = 576 + 96 * (c // 6)
        return w_ref[:, top : top + 96, c % 6 * BLOCK : (c % 6 + 1) * BLOCK].reshape(INNER, BLOCK)

    def save(c):
        cols = pl.ds(c * BLOCK, BLOCK)
        return pltpu.make_async_copy(out_ref.at[:, cols], saved_ref.at[micro, :, cols], out_sem.at[c])

    @pl.when((mine >= 0) & (mine < micros))
    def _():
        @pl.when(at_ref[0] == 0)
        def _():
            copy = pltpu.make_async_copy(tokens_ref.at[micro], x_ref, sem.at[0])
            copy.start()
            copy.wait()

        @pl.when(at_ref[0] != 0)
        def _():
            x_ref[...] = incoming_ref[...]

        code_c = code_c_ref[micro]
        code_r = code_r_ref[micro]
        normed_ref[...] = group_normed(x_ref[...], code_c, code_r, gain_ref[...], bias_ref[...], groups_ref[...])
        head_r = lax.broadcasted_iota(jnp.int32, (BLOCK, BLOCK), 0) // HD
        head_c = lax.broadcasted_iota(jnp.int32, (BLOCK, BLOCK), 1) // HD
        same = head_r == head_c
        one = same.astype(BF)
        zero = jnp.zeros((BLOCK, BLOCK), BF)
        allowed = []
        for seq in range(PER):
            own = code_c[seq * LEN : (seq + 1) * LEN]
            tile = ((own == code_r[:, seq * LEN : (seq + 1) * LEN]) & (own >= 0)).astype(F32)
            allowed.append(jnp.concatenate([tile] * 4, axis=1))
        dropped = (code_c < 0).astype(F32)
        normed = normed_ref[...]
        def project(j):
            return dot(normed, wq(0, j)), dot(normed, wq(1, j)), dot(normed, wq(2, j))

        def attend(j, query, key, value):
            pair = jnp.concatenate([query, key], axis=0)
            square = dot((pair * pair).astype(BF), one) * (1.0 / HD)
            pair = pair * lax.rsqrt(square + 1e-06)
            query = (pair[:ROWS] * (1.0 / math.sqrt(HD))).astype(BF)
            key = pair[ROWS:].astype(BF)
            value = value.astype(BF)
            for seq in range(PER):
                rows = slice(seq * LEN, (seq + 1) * LEN)
                key_bd = jnp.where(same, jnp.concatenate([key[rows]] * 4, axis=0), zero)
                value_bd = jnp.where(same, jnp.concatenate([value[rows]] * 4, axis=0), zero)
                expo = (jnp.exp(dot_nt(query[rows], key_bd)) * allowed[seq]).astype(BF)
                both = dot(expo, jnp.concatenate([value_bd, one], axis=1))
                found = both[:, :BLOCK] / (both[:, BLOCK:] + dropped[rows])
                attended_ref[rows, j * BLOCK : (j + 1) * BLOCK] = found.astype(BF)

        ready = project(0)
        for j in range(6):
            following = project(j + 1) if j < 5 else None
            attend(j, *ready)
            ready = following
        attended = attended_ref[...]
        for j in range(6):
            for c in (j, j + 6):
                cols = slice(c * BLOCK, (c + 1) * BLOCK)
                out_ref[:, cols] = (x_ref[:, cols].astype(F32) + dot(attended, wo(c))).astype(BF)
                save(c).start()
        for c in range(12):
            save(c).wait()


def tick(now, at, incoming, tokens, code_c, code_r, gain, bias, groups, weights, saved):
    whole = pl.BlockSpec(memory_space=pltpu.VMEM)
    anywhere = pl.BlockSpec(memory_space=pl.ANY)
    scalar = pl.BlockSpec(memory_space=pltpu.SMEM)
    return pl.pallas_call(
        functools.partial(tick_kernel, now),
        out_shape=(pltpu.VMEM((ROWS, D), BF), jax.ShapeDtypeStruct(tokens.shape, BF)),
        in_specs=[scalar, whole, anywhere, whole, whole, whole, whole, whole, whole] + [anywhere] * len(saved),
        out_specs=(whole, anywhere),
        scratch_shapes=[
            pltpu.VMEM((ROWS, D), BF),
            pltpu.VMEM((ROWS, D), BF),
            pltpu.VMEM((ROWS, INNER), BF),
            pltpu.SemaphoreType.DMA((1,)),
            pltpu.SemaphoreType.DMA((12,)),
        ],
        input_output_aliases={9: 1} if saved else {},
        compiler_params=pltpu.CompilerParams(vmem_limit_bytes=18 << 20),
    )(at, incoming, tokens, code_c, code_r, gain, bias, groups, weights, *saved)


SIDE = 4


def moved(value, dz, dx):
    steps = [
        (z * SIDE + x, (z + dz) % SIDE * SIDE + (x + dx) % SIDE) for z in range(SIDE) for x in range(SIDE)
    ]
    return lax.ppermute(value, "dp", steps)


def ring(own, dz, dx):
    before = [moved(half, dz, dx) for half in own]
    after = [moved(half, -dz, -dx) for half in reversed(own)][::-1]
    return [own, before, after, [moved(before[0], dz, dx), moved(after[1], -dz, -dx)]]


STEPS = (0, SIDE - 1, 1, 2)


def load_kernel(fars, at_ref, *refs):
    pieces, (out_ref, sem) = refs[: 4 * len(fars)], refs[-2:]
    rows = out_ref.shape[1] // 2
    place = (at_ref[0] // SIDE, at_ref[0] % SIDE)
    copies = []
    for at, far in enumerate(fars):
        for color in range(2):
            for near in range(4):
                source = pieces[4 * at + 2 * color + near // 2].at[pl.ds(near % 2 * rows, rows)]
                z = place[0] + STEPS[(far, near)[color]]
                x = place[1] + STEPS[(near, far)[color]]
                target = out_ref.at[z % SIDE * SIDE + x % SIDE, pl.ds(color * rows, rows)]
                copies.append(pltpu.make_async_copy(source, target, sem.at[len(copies)]))
    for copy in copies:
        copy.start()
    for copy in copies:
        copy.wait()


def loaded(shape, fars, blocks, held):
    pieces = [half for far in fars for color in range(2) for half in blocks[color][far]]
    return pl.pallas_call(
        functools.partial(load_kernel, fars),
        out_shape=pltpu.VMEM(shape, BF),
        in_specs=[pl.BlockSpec(memory_space=pltpu.SMEM)]
        + [pl.BlockSpec(memory_space=pl.ANY)] * len(pieces)
        + [pl.BlockSpec(memory_space=pltpu.VMEM)] * len(held),
        out_specs=pl.BlockSpec(memory_space=pltpu.VMEM),
        scratch_shapes=[pltpu.SemaphoreType.DMA((8 * len(fars),))],
        input_output_aliases={1 + len(pieces): 0} if held else {},
        compiler_params=pltpu.CompilerParams(vmem_limit_bytes=18 << 20),
    )(lax.axis_index("dp").reshape(1), *pieces, *held)


def gathered(packed):
    quarter = packed.shape[0] // 4
    halves = []
    for color, (dz, dx) in enumerate(((0, 1), (1, 0))):
        top = 2 * color * quarter
        own = [packed[top : top + quarter], packed[top + quarter : top + 2 * quarter]]
        own, before, after, last = ring(own, dz, dx)
        halves.append([jnp.concatenate(own + before), jnp.concatenate(after + last)])
    halves = lax.optimization_barrier(halves)
    blocks = [ring(halves[0], 1, 0), ring(halves[1], 0, 1)]
    shape = (SIDE * SIDE, *packed.shape)
    held = loaded(shape, (0, 1, 2), blocks, [])
    return pltpu.with_memory_space_constraint(
        loaded(shape, (3,), blocks, [pltpu.with_memory_space_constraint(held, pltpu.VMEM)]), pltpu.VMEM
    )


def local(tokens, segments, keep_mask, norm_gain, norm_bias, w_qkv, w_out):
    section = lax.axis_index("pipe")
    sections = lax.axis_size("pipe")
    micro = tokens.shape[0] // PER
    qkv, out = w_qkv[0], w_out[0]
    packed = jnp.concatenate(
        [qkv[:, i * INNER : (i + 1) * INNER] for i in range(3)] + [out[:, i * INNER : (i + 1) * INNER] for i in range(2)],
        axis=0,
    )
    weights = gathered(packed)
    place = lax.broadcasted_iota(jnp.int32, segments.shape, 0) % PER * IMGS
    code = jnp.where(keep_mask > 0, segments + place, -1)
    code_c = code.reshape(micro, ROWS, 1)
    code_r = code.reshape(micro, 1, ROWS)
    owner = lax.broadcasted_iota(jnp.int32, (GROUPS * 3, D), 0) % GROUPS
    groups = (lax.broadcasted_iota(jnp.int32, (GROUPS * 3, D), 1) // WIDTH == owner).astype(BF)
    shaped = tokens.reshape(micro, ROWS, D)
    saved = []
    incoming = shaped[0]
    steps = [(i, i + 1) for i in range(sections - 1)]
    at = section.reshape(1)
    fixed = [
        pltpu.with_memory_space_constraint(part, pltpu.VMEM) for part in (code_c, code_r, norm_gain, norm_bias, groups)
    ]

    for now in range(micro + sections - 1):
        result, *saved = tick(now, at, incoming, shaped, *fixed, weights, saved)
        if now < micro + sections - 2:
            incoming = pltpu.with_memory_space_constraint(lax.ppermute(result, "pipe", steps), pltpu.VMEM)
    return saved[0].reshape((1,) + tokens.shape)


def solution(mesh):
    placed = (
        P("dp", None, None),
        P("dp", None),
        P("dp", None),
        P("pipe", None),
        P("pipe", None),
        P("pipe", "dp", None),
        P("pipe", "dp", None),
    )
    return jax.shard_map(
        local, mesh=mesh, in_specs=placed, out_specs=P("pipe", "dp", None, None), check_vma=False
    )
```
